32 devices in a mesh: seq: 4 (over z), cfg: 2 (over core), fsdp: 4 (over y, x).
Axes of the slice: x: 2, y: 2, z: 4, core: 2. Of those that a mesh axis runs over, the one named last changes fastest.
Arguments:
- q_raw: bfloat16 [4, 2, 512, 2560], P('fsdp', 'cfg', 'seq'), may hold values from -600 to 600
- k_raw: bfloat16 [4, 2, 512, 2560], P('fsdp', 'cfg', 'seq'), may hold values from -600 to 600
- value_in: bfloat16 [4, 2, 512, 2560], P('fsdp', 'cfg', 'seq'), may hold values from -6 to 6
- cotangent: bfloat16 [4, 2, 512, 2560], P('fsdp', 'cfg', 'seq'), may hold values from -45 to 45
- q_gain: float32 [2560], P('fsdp'), may hold values from 0.5 to 1.5
- k_gain: float32 [2560], P('fsdp'), may hold values from 0.5 to 1.5
- tile_lists: int32 [20, 8, 6], replicated, may hold values from -1 to 7, as said below
Outputs:
- q_grad: bfloat16 [4, 2, 512, 2560], P('fsdp', 'cfg', 'seq')
- k_grad: bfloat16 [4, 2, 512, 2560], P('fsdp', 'cfg', 'seq')
- v_grad: bfloat16 [4, 2, 512, 2560], P('fsdp', 'cfg', 'seq')
- q_gain_grad: float32 [2560], P('fsdp')
- k_gain_grad: float32 [2560], P('fsdp')
The draws below stay inside these ranges and needn't reach their ends.
Inputs may be any that keep to these rules, and one draw needn't show every extreme that they name: `tile_lists`: row h, a lists distinct tiles in increasing order, then -1 entries. Tile a's own slab (tile index // 2) is always listed whole; every listed tile's slab differs from tile a's slab by at most 1; some row holds 6 tiles.
All inputs are finite; a program needn't handle non-finite values.
Results may differ from the reference program's by a relative error of at most 0.039.
Values may be sent and summed in bfloat16 or wider, within the bound.
A program may use at most 64 MiB of HBM per device.

```python
import math
import jax
import jax.numpy as jnp
from jax import lax

HEADS = 20
HEAD_DIM = 128
TILE = 64
TILES_DEV = 2
WIDTH = 2560
TOKENS = 512
CLIPS = 4


def drawn_pair(key):
    base_key = jax.random.fold_in(key, 11)
    split_keys = jax.random.split(base_key, 5)
    shape = (CLIPS, 2, TOKENS, HEADS * HEAD_DIM)
    column_scale = jnp.exp(jax.random.uniform(split_keys[0], (HEADS * HEAD_DIM,), jnp.float32) * jnp.log(10.0))
    query_rows = jnp.exp(jax.random.uniform(split_keys[1], (CLIPS, 2, TOKENS, 1), jnp.float32) * jnp.log(10.0))
    key_rowscale = jnp.exp(jax.random.uniform(split_keys[2], (CLIPS, 2, TOKENS, 1), jnp.float32) * jnp.log(10.0))
    query_base = jax.random.truncated_normal(split_keys[3], -5.0, 5.0, shape, jnp.float32) * column_scale
    key_base = jax.random.truncated_normal(split_keys[4], -5.0, 5.0, shape, jnp.float32) * column_scale
    return (query_base * query_rows, key_base * key_rowscale)


def draw_q_raw(key, part):
    return drawn_pair(key)[0].astype(jnp.bfloat16)


def draw_k_raw(key, part):
    return drawn_pair(key)[1].astype(jnp.bfloat16)


def draw_cotangent(key, part):
    shape = (CLIPS, 2, TOKENS, HEADS * HEAD_DIM)
    first_key = jax.random.fold_in(jax.random.fold_in(key, 7), 0)
    position = jnp.arange(TOKENS, dtype=jnp.float32) / TOKENS
    result = jax.random.truncated_normal(first_key, -5.0, 5.0, shape, jnp.float32) * (3.0 ** position)[:, None]
    return result.astype(jnp.bfloat16)


def draw_tile_lists(key, part):
    tile_count = TOKENS // TILE
    list_len = 3 * TILES_DEV
    split_keys = jax.random.split(jax.random.fold_in(key, 5), 4)
    level = jax.random.randint(split_keys[0], (HEADS, 1), 0, 5)
    wide = (jax.random.randint(split_keys[1], (HEADS, tile_count), 0, 4) < level).astype(jnp.int32)
    force_head = jax.random.randint(split_keys[2], (), 0, HEADS)
    force_tile = jax.random.randint(split_keys[3], (), TILES_DEV, tile_count - TILES_DEV)
    wide = wide.at[force_head, force_tile].set(1)
    query_slab = jnp.arange(tile_count, dtype=jnp.int32) // TILES_DEV
    offsets = jnp.arange(list_len, dtype=jnp.int32)
    candidate = (query_slab[:, None] - 1) * TILES_DEV + offsets[None, :]
    candidate_slab = jnp.floor_divide(candidate, TILES_DEV)
    inside = (candidate >= 0) & (candidate < tile_count)
    same_slab = candidate_slab == query_slab[:, None]
    is_valid = inside[None] & (same_slab[None] | (wide[:, :, None] == 1))
    order_key = jnp.where(is_valid, 0, list_len) + offsets
    order = jnp.argsort(order_key, axis=-1, stable=True)
    marked = jnp.where(is_valid, candidate[None], -1)
    return jnp.take_along_axis(marked, order, axis=-1).astype(jnp.int32)


def level_of(stream_key, extent, pieces, low, largest):
    def one(dim, shards_of):
        steps = jax.random.uniform(jax.random.fold_in(jax.random.fold_in(stream_key, 6), dim), (shards_of,), jnp.float32, low / len(pieces), largest / len(pieces))
        return jnp.repeat(jnp.exp(steps), extent[dim] // shards_of).reshape((-1,) + (1,) * (len(extent) - dim - 1))

    factor_of = one(*pieces[0])
    for cut in pieces[1:]:
        factor_of = factor_of * one(*cut)
    return factor_of


def gaussian(own_key, shape, width, limit, pieces=(), held_as=jnp.bfloat16):
    factor_of = level_of(own_key, shape, pieces, -0.22, 0.18) if pieces else 1.0
    drawn = jax.random.normal(own_key, shape, jnp.float32) * width * factor_of
    return jnp.minimum(jnp.maximum(drawn, -limit), limit).astype(held_as)


def setup_inputs(seed: int = 0) -> dict:
    seeds = jax.random.split(jax.random.key(seed), 8)
    return {
        "q_raw": draw_q_raw(jax.random.fold_in(seeds[7], 71), 0),
        "k_raw": draw_k_raw(jax.random.fold_in(seeds[7], 71), 0),
        "value_in": gaussian(seeds[2], (CLIPS, 2, TOKENS, WIDTH), 1.0, 6.0, ((0, 4), (1, 2), (2, 4))),
        "cotangent": draw_cotangent(jax.random.fold_in(seeds[7], 71), 0),
        "q_gain": jnp.clip(1.0 + 0.1 * jax.random.normal(seeds[4], (WIDTH,), jnp.float32), 0.5, 1.5),
        "k_gain": jnp.clip(1.0 + 0.1 * jax.random.normal(seeds[5], (WIDTH,), jnp.float32), 0.5, 1.5),
        "tile_lists": draw_tile_lists(jax.random.fold_in(seeds[7], 71), 0),
    }


def norm_rows(raw_rows, gain_full):
    row_values = raw_rows.astype(jnp.float32)
    row_scale = jnp.sqrt(lax.optimization_barrier(jnp.mean(row_values * row_values, axis=-1, keepdims=True)) + 1e-06)
    return (row_values, row_scale, (row_values / row_scale * gain_full).astype(jnp.bfloat16))

def norm_back(row_values, row_scale, gain_full, normed_grad):
    grad_values = normed_grad.astype(jnp.float32)
    upstream = grad_values * gain_full
    inner_sum = lax.optimization_barrier(jnp.sum(row_values * upstream, axis=-1, keepdims=True))
    feature_count = row_values.shape[-1]
    input_grad = upstream / row_scale - row_values * inner_sum / (feature_count * row_scale ** 3)
    gain_part = lax.optimization_barrier(jnp.sum(grad_values * row_values / row_scale, axis=0))
    return (input_grad.astype(jnp.bfloat16), gain_part)

def head_pass(queries, key_tiles, value_tiles, cotangent_tiles, tile_rows):
    tile_count, tile_len, head_dim = queries.shape
    list_len = tile_rows.shape[1]
    score_scale = 1.0 / math.sqrt(head_dim)
    is_valid = tile_rows >= 0
    safe_index = jnp.where(is_valid, tile_rows, 0)
    key_rows = key_tiles[safe_index].reshape(tile_count, list_len * tile_len, head_dim).astype(jnp.float32)
    value_rows = value_tiles[safe_index].reshape(tile_count, list_len * tile_len, head_dim).astype(jnp.float32)
    query_values = queries.astype(jnp.float32)
    cotangent_values = cotangent_tiles.astype(jnp.float32)
    key_mask = jnp.repeat(is_valid, tile_len, axis=1)[:, None, :]
    scores = jnp.einsum('aqd,akd->aqk', query_values, key_rows) * score_scale
    scores = jnp.where(key_mask, scores, -jnp.inf)
    row_max = lax.optimization_barrier(jnp.max(scores, axis=2, keepdims=True))
    expo_values = jnp.exp(scores - row_max)
    weights = expo_values / lax.optimization_barrier(jnp.sum(expo_values, axis=2, keepdims=True))
    weights_low = weights.astype(jnp.bfloat16).astype(jnp.float32)
    attn_out = jnp.einsum('aqk,akd->aqd', weights_low, value_rows).astype(jnp.bfloat16)
    delta = lax.optimization_barrier(jnp.sum(cotangent_values * attn_out.astype(jnp.float32), axis=2, keepdims=True))
    prob_grad = jnp.einsum('aqd,akd->aqk', cotangent_values, value_rows)
    score_grad = (weights * (prob_grad - delta) * score_scale).astype(jnp.bfloat16).astype(jnp.float32)
    query_grad = jnp.einsum('aqk,akd->aqd', score_grad, key_rows)
    key_part = jnp.einsum('aqk,aqd->akd', score_grad, query_values).reshape(tile_count, list_len, tile_len, head_dim)
    value_part = jnp.einsum('aqk,aqd->akd', weights_low, cotangent_values).reshape(tile_count, list_len, tile_len, head_dim)
    target = jnp.where(is_valid, tile_rows, tile_count)
    key_grad = jnp.zeros((tile_count, tile_len, head_dim), jnp.float32).at[target].add(key_part, mode='drop')
    value_grad = jnp.zeros((tile_count, tile_len, head_dim), jnp.float32).at[target].add(value_part, mode='drop')
    return (query_grad.astype(jnp.bfloat16), key_grad.astype(jnp.bfloat16), value_grad.astype(jnp.bfloat16))

def reference(q_raw, k_raw, value_in, cotangent, q_gain, k_gain, tile_lists):
    clip_count = q_raw.shape[0]
    token_count = q_raw.shape[2]
    tile_count = token_count // TILE

    def head_major(rows):
        return rows.reshape(tile_count, TILE, HEADS, HEAD_DIM).transpose(2, 0, 1, 3)

    def token_major(tiles):
        return tiles.transpose(1, 2, 0, 3).reshape(token_count, HEADS * HEAD_DIM)

    def one_pass(inputs):
        query_raw, key_raw, value_rows, cotangent_rows = inputs
        q_values, q_scale, q_normed = norm_rows(query_raw, q_gain)
        k_values, k_scale, k_normed = norm_rows(key_raw, k_gain)
        grads = jax.vmap(head_pass)(head_major(q_normed), head_major(k_normed), head_major(value_rows), head_major(cotangent_rows), tile_lists)
        q_out, q_part = norm_back(q_values, q_scale, q_gain, token_major(grads[0]))
        k_out, k_part = norm_back(k_values, k_scale, k_gain, token_major(grads[1]))
        return (q_out, k_out, token_major(grads[2]), q_part, k_part)

    def flatten(array):
        return array.reshape((clip_count * 2,) + array.shape[2:])
    results = lax.map(one_pass, (flatten(q_raw), flatten(k_raw), flatten(value_in), flatten(cotangent)))
    full_shape = q_raw.shape
    divisor = 2.0 * clip_count
    return (results[0].reshape(full_shape), results[1].reshape(full_shape), results[2].reshape(full_shape), lax.optimization_barrier(jnp.sum(results[3], axis=0)) / divisor, lax.optimization_barrier(jnp.sum(results[4], axis=0)) / divisor)
```

```python
import functools
import math

import jax
import jax.numpy as jnp
from jax import lax
from jax.experimental import pallas as pl
from jax.experimental.pallas import tpu as pltpu
from jax.sharding import PartitionSpec as P

HEAD_DIM = 128
TILE = 64
LOW = -1e30
MESH = pl.DeviceIdType.MESH
NT = (((1,), (1,)), ((), ()))
NN = (((1,), (0,)), ((), ()))
TN = (((0,), (0,)), ((), ()))


def dot(a, b, dims):
    return lax.dot_general(a, b, dims, preferred_element_type=jnp.float32)


def fused(
    sizes,
    q_ref,
    k_ref,
    v_ref,
    c_ref,
    gain_ref,
    mask_ref,
    dq_ref,
    dk_ref,
    dv_ref,
    gsum_ref,
    qn,
    kn,
    hq,
    hc,
    s_buf,
    p_buf,
    stat,
    stat_in,
    fin,
    fin_in,
    dq_own,
    dq_send,
    dq_in,
    gslots,
    gp,
    fslots,
    gp2,
    cslots,
    hc_send,
    hc_recv,
    hq_send,
    hq_recv,
    st_send,
    st_recv,
    fin_send,
    fin_recv,
    dq_ssem,
    dq_rsem,
    g_send,
    g_recv,
    f_send,
    f_recv,
    x_send,
    x_recv,
):
    seq_n, cfg_n, fsdp_n, heads, group_heads = sizes
    rows, width = q_ref.shape
    groups = heads // group_heads
    group_width = group_heads * HEAD_DIM
    slab_tiles = rows // TILE
    score_scale = 1.0 / math.sqrt(HEAD_DIM)
    z = lax.axis_index("seq")
    c = lax.axis_index("cfg")
    f = lax.axis_index("fsdp")
    place = z * cfg_n + c
    here = (z > 0, z < seq_n - 1)
    there = (z - 1, z + 1)

    fsdp_peers = [lax.rem(f + i, fsdp_n) for i in range(1, fsdp_n)]
    row_peers = [lax.rem(place + i, seq_n * cfg_n) for i in range(1, seq_n * cfg_n)]

    def row_id(peer):
        return {"seq": lax.div(peer, cfg_n), "cfg": lax.rem(peer, cfg_n)}

    barrier = pltpu.get_barrier_semaphore()
    for peer in fsdp_peers:
        pl.semaphore_signal(barrier, inc=1, device_id={"fsdp": peer}, device_id_type=MESH)
    for peer in row_peers:
        pl.semaphore_signal(barrier, inc=1, device_id=row_id(peer), device_id_type=MESH)
    pl.semaphore_wait(barrier, len(fsdp_peers) + len(row_peers))

    def outgoing(side, src, dst, send, recv, tail=(), sem_tail=()):
        return pltpu.make_async_remote_copy(
            src_ref=src,
            dst_ref=dst.at[(1 - side,) + tail],
            send_sem=send.at[(side,) + sem_tail],
            recv_sem=recv.at[(1 - side,) + sem_tail],
            device_id={"seq": there[side]},
            device_id_type=MESH,
        )

    def incoming(side, src, dst, send, recv, tail=(), sem_tail=()):
        return pltpu.make_async_remote_copy(
            src_ref=src,
            dst_ref=dst.at[(side,) + tail],
            send_sem=send.at[(side,) + sem_tail],
            recv_sem=recv.at[(side,) + sem_tail],
            device_id={"seq": there[side]},
            device_id_type=MESH,
        )

    for side in range(2):

        @pl.when(here[side])
        def _(side=side):
            outgoing(side, c_ref, hc, hc_send, hc_recv).start()

    def peer_copy(src, slots, slot, send_slot, send, recv, target):
        return pltpu.make_async_remote_copy(
            src_ref=src,
            dst_ref=slots.at[slot],
            send_sem=send.at[send_slot],
            recv_sem=recv.at[slot],
            device_id=target,
            device_id_type=MESH,
        )

    for peer in fsdp_peers:
        peer_copy(gain_ref, gslots, f, peer, g_send, g_recv, {"fsdp": peer}).start()
    gslots[f] = gain_ref[...]

    for side in range(2):

        @pl.when(jnp.logical_not(here[side]))
        def _(side=side):
            hq[side] = jnp.zeros((rows, width), jnp.bfloat16)
            hc[side] = jnp.zeros((rows, width), jnp.bfloat16)
            dq_in[side] = jnp.zeros((rows, width), jnp.bfloat16)
            fin_in[side] = jnp.zeros((3, heads, rows), jnp.float32)
            stat_in[side, 0] = jnp.full((heads, rows), LOW, jnp.float32)
            stat_in[side, 1:3] = jnp.zeros((2, heads, rows), jnp.float32)

    def columns(h):
        return pl.ds(pl.multiple_of(h * HEAD_DIM, HEAD_DIM), HEAD_DIM)

    def group_columns(g):
        return pl.ds(pl.multiple_of(g * group_width, HEAD_DIM), group_width)

    def square_step(h, sums):
        q_block = q_ref[:, columns(h)].astype(jnp.float32)
        k_block = k_ref[:, columns(h)].astype(jnp.float32)
        return (sums[0] + q_block * q_block, sums[1] + k_block * k_block)

    zeros = jnp.zeros((rows, HEAD_DIM), jnp.float32)
    q_sq, k_sq = lax.fori_loop(0, heads, square_step, (zeros, zeros))
    q_scale = jnp.sqrt(jnp.sum(q_sq, axis=1, keepdims=True) / width + 1e-06)
    k_scale = jnp.sqrt(jnp.sum(k_sq, axis=1, keepdims=True) / width + 1e-06)
    q_inv = 1.0 / q_scale
    k_inv = 1.0 / k_scale

    for peer in fsdp_peers:
        peer_copy(gain_ref, gslots, peer, peer, g_send, g_recv, {"fsdp": peer}).wait()
    gains = gslots[0]
    for i in range(1, fsdp_n):
        gains = gains + gslots[i]
    gslots[0] = gains

    def head_gain(row, h):
        return gslots[0, row : row + 1, columns(h)]

    @pl.loop(0, groups)
    def _(g):
        for j in range(group_heads):
            h = g * group_heads + j
            cols = columns(h)
            qn[:, cols] = (q_ref[:, cols].astype(jnp.float32) * q_inv * head_gain(0, h)).astype(
                jnp.bfloat16
            )
            kn[:, cols] = (k_ref[:, cols].astype(jnp.float32) * k_inv * head_gain(1, h)).astype(
                jnp.bfloat16
            )

    def q_chunk(make, side, g):
        cols = group_columns(g)
        return make(
            side, qn.at[:, cols], hq, hq_send, hq_recv, (slice(None), cols), (g,)
        )

    for side in range(2):

        @pl.when(here[side])
        def _(side=side):
            @pl.loop(0, groups)
            def _(g):
                q_chunk(outgoing, side, g).start()

    def stats_of(slot, h, queries, cots):
        cols = columns(h)
        scores = dot(kn[:, cols], queries, NT) * score_scale
        probs = dot(v_ref[:, cols], cots, NT)
        flags = mask_ref[h]
        live = (
            jnp.concatenate(
                [
                    jnp.broadcast_to(flags[slot * slab_tiles + t][None, :], (TILE, rows))
                    for t in range(slab_tiles)
                ],
                axis=0,
            )
            > 0.5
        )
        scores = jnp.where(live, scores, LOW)
        top = jnp.max(scores, axis=0, keepdims=True)
        expo = jnp.where(live, jnp.exp(scores - top), 0.0)
        s_buf[slot, h] = scores
        p_buf[slot, h] = probs
        stat[slot, 0, pl.ds(h, 1), :] = top
        stat[slot, 1, pl.ds(h, 1), :] = jnp.sum(expo, axis=0, keepdims=True)
        stat[slot, 2, pl.ds(h, 1), :] = jnp.sum(expo * probs, axis=0, keepdims=True)

    @pl.loop(0, groups)
    def _(g):
        for j in range(group_heads):
            h = g * group_heads + j
            stats_of(1, h, qn[:, columns(h)], c_ref[:, columns(h)])

    for side in range(2):

        @pl.when(here[side])
        def _(side=side):
            incoming(side, c_ref, hc, hc_send, hc_recv).wait_recv()

    @pl.loop(0, groups)
    def _(g):
        for side in range(2):

            @pl.when(here[side])
            def _(side=side):
                q_chunk(incoming, side, g).wait_recv()

        for j in range(group_heads):
            h = g * group_heads + j
            for side in range(2):
                stats_of(2 * side, h, hq[side, :, columns(h)], hc[side, :, columns(h)])

    for side in range(2):

        @pl.when(here[side])
        def _(side=side):
            outgoing(side, stat.at[2 * side], stat_in, st_send, st_recv).start()

    for side in range(2):

        @pl.when(here[side])
        def _(side=side):
            incoming(side, stat.at[2 * side], stat_in, st_send, st_recv).wait_recv()

    tops = (stat_in[0, 0], stat[1, 0], stat_in[1, 0])
    top = jnp.maximum(jnp.maximum(tops[0], tops[1]), tops[2])
    factors = [jnp.exp(part - top) for part in tops]
    total = stat_in[0, 1] * factors[0] + stat[1, 1] * factors[1] + stat_in[1, 1] * factors[2]
    weighted = stat_in[0, 2] * factors[0] + stat[1, 2] * factors[1] + stat_in[1, 2] * factors[2]
    inverse = 1.0 / total
    fin[0] = top
    fin[1] = inverse
    fin[2] = weighted * inverse

    for side in range(2):

        @pl.when(here[side])
        def _(side=side):
            outgoing(side, fin, fin_in, fin_send, fin_recv).start()

    for side in range(2):

        @pl.when(here[side])
        def _(side=side):
            incoming(side, fin, fin_in, fin_send, fin_recv).wait_recv()

    def back_of(slot, h, final, queries, cots):
        weights = jnp.exp(s_buf[slot, h] - final(0, h)) * final(1, h)
        grads = (weights * (p_buf[slot, h] - final(2, h)) * score_scale).astype(jnp.bfloat16)
        return (
            dot(grads, kn[:, columns(h)], TN),
            dot(grads, queries, NN),
            dot(weights.astype(jnp.bfloat16), cots, NN),
        )

    def dq_chunk(make, side, g):
        cols = group_columns(g)
        return make(
            side,
            dq_send.at[side, :, cols],
            dq_in,
            dq_ssem,
            dq_rsem,
            (slice(None), cols),
            (g,),
        )

    @pl.loop(0, groups)
    def _(g):
        for j in range(group_heads):
            h = g * group_heads + j
            cols = columns(h)
            k_sum = None
            v_sum = None
            for side in range(2):
                q_part, k_part, v_part = back_of(
                    2 * side,
                    h,
                    lambda i, n, side=side: fin_in[side, i, pl.ds(n, 1), :],
                    hq[side, :, cols],
                    hc[side, :, cols],
                )
                dq_send[side, :, cols] = q_part.astype(jnp.bfloat16)
                k_sum = k_part if k_sum is None else k_sum + k_part
                v_sum = v_part if v_sum is None else v_sum + v_part
            q_part, k_part, v_part = back_of(
                1, h, lambda i, n: fin[i, pl.ds(n, 1), :], qn[:, cols], c_ref[:, cols]
            )
            dq_own[:, cols] = q_part
            dk_ref[:, cols] = (k_sum + k_part).astype(jnp.bfloat16)
            dv_ref[:, cols] = (v_sum + v_part).astype(jnp.bfloat16)
        for side in range(2):

            @pl.when(here[side])
            def _(side=side):
                dq_chunk(outgoing, side, g).start()

    def norm_back(row, raw_ref, grad_of, out_ref, inverse_scale):
        def first(h, inner):
            cols = columns(h)
            raw = raw_ref[:, cols].astype(jnp.float32)
            grad = grad_of(h)
            gp[row : row + 1, cols] = jnp.sum(grad * (raw * inverse_scale), axis=0, keepdims=True)
            return inner + raw * (grad * head_gain(row, h))

        inner = lax.fori_loop(0, heads, first, zeros)
        inner = jnp.sum(inner, axis=1, keepdims=True)
        ratio = inner / width * (inverse_scale * inverse_scale * inverse_scale)

        @pl.loop(0, heads)
        def _(h):
            cols = columns(h)
            raw = raw_ref[:, cols].astype(jnp.float32)
            grad = out_ref[:, cols].astype(jnp.float32)
            out_ref[:, cols] = (
                grad * head_gain(row, h) * inverse_scale - raw * ratio
            ).astype(jnp.bfloat16)

    norm_back(1, k_ref, lambda h: dk_ref[:, columns(h)].astype(jnp.float32), dk_ref, k_inv)

    @pl.loop(0, groups)
    def _(g):
        for side in range(2):

            @pl.when(here[side])
            def _(side=side):
                dq_chunk(incoming, side, g).wait_recv()

    def joined(h):
        cols = columns(h)
        total_grad = (
            dq_own[:, cols]
            + dq_in[0, :, cols].astype(jnp.float32)
            + dq_in[1, :, cols].astype(jnp.float32)
        ).astype(jnp.bfloat16)
        dq_ref[:, cols] = total_grad
        return total_grad.astype(jnp.float32)

    norm_back(0, q_ref, joined, dq_ref, q_inv)

    for peer in row_peers:
        peer_copy(gp, cslots, place, peer, x_send, x_recv, row_id(peer)).start()
    cslots[place] = gp[...]
    for peer in row_peers:
        peer_copy(gp, cslots, peer, peer, x_send, x_recv, row_id(peer)).wait()
    part = cslots[0]
    for i in range(1, seq_n * cfg_n):
        part = part + cslots[i]
    gp2[...] = part
    for peer in fsdp_peers:
        peer_copy(gp2, fslots, f, peer, f_send, f_recv, {"fsdp": peer}).start()
    fslots[f] = part
    for peer in fsdp_peers:
        peer_copy(gp2, fslots, peer, peer, f_send, f_recv, {"fsdp": peer}).wait()
    part = fslots[0]
    for i in range(1, fsdp_n):
        part = part + fslots[i]
    gsum_ref[...] = part / (2.0 * fsdp_n)

    for side in range(2):

        @pl.when(here[side])
        def _(side=side):
            outgoing(side, c_ref, hc, hc_send, hc_recv).wait_send()
            outgoing(side, stat.at[2 * side], stat_in, st_send, st_recv).wait_send()
            outgoing(side, fin, fin_in, fin_send, fin_recv).wait_send()

            @pl.loop(0, groups)
            def _(g):
                q_chunk(outgoing, side, g).wait_send()
                dq_chunk(outgoing, side, g).wait_send()


def on_device(q_raw, k_raw, value_in, cotangent, q_gain, k_gain, tile_lists):
    seq_n, cfg_n, fsdp_n = (lax.axis_size(name) for name in ("seq", "cfg", "fsdp"))
    rows, width = q_raw.shape[2:]
    heads = width // HEAD_DIM
    slab_tiles = rows // TILE
    share = q_gain.shape[0]
    group_heads = next(n for n in (4, 3, 2, 1) if heads % n == 0)
    groups = heads // group_heads

    owner = lax.broadcasted_iota(jnp.int32, (2, width), 1) // share
    both = jnp.stack([jnp.tile(q_gain, fsdp_n), jnp.tile(k_gain, fsdp_n)])
    placed = jnp.where(owner == lax.axis_index("fsdp"), both, 0.0)

    slab = lax.axis_index("seq")
    padded = jnp.pad(
        tile_lists, ((0, 0), (slab_tiles, slab_tiles), (0, 0)), constant_values=-1
    )
    near = lax.dynamic_slice_in_dim(padded, slab * slab_tiles, 3 * slab_tiles, 1)
    key_tiles = slab * slab_tiles + jnp.arange(slab_tiles, dtype=jnp.int32)
    listed = jnp.any(near[:, :, :, None] == key_tiles, axis=2)
    listed = listed.reshape(heads, 3, slab_tiles, slab_tiles).swapaxes(2, 3)
    flags = jnp.repeat(listed, TILE, axis=3).reshape(heads, 3 * slab_tiles, rows)
    flags = flags.astype(jnp.float32)

    bf16, f32 = jnp.bfloat16, jnp.float32
    dma = pltpu.SemaphoreType.DMA
    places = seq_n * cfg_n
    vmem = pl.BlockSpec(memory_space=pltpu.VMEM)
    grad = jax.ShapeDtypeStruct((rows, width), bf16)
    q_out, k_out, v_out, gain_sums = pl.pallas_call(
        functools.partial(fused, (seq_n, cfg_n, fsdp_n, heads, group_heads)),
        out_shape=(grad, grad, grad, jax.ShapeDtypeStruct((2, width), f32)),
        in_specs=[vmem] * 6,
        out_specs=(vmem,) * 4,
        scratch_shapes=[
            pltpu.VMEM((rows, width), bf16),
            pltpu.VMEM((rows, width), bf16),
            pltpu.VMEM((2, rows, width), bf16),
            pltpu.VMEM((2, rows, width), bf16),
            pltpu.VMEM((3, heads, rows, rows), f32),
            pltpu.VMEM((3, heads, rows, rows), f32),
            pltpu.VMEM((3, 3, heads, rows), f32),
            pltpu.VMEM((2, 3, heads, rows), f32),
            pltpu.VMEM((3, heads, rows), f32),
            pltpu.VMEM((2, 3, heads, rows), f32),
            pltpu.VMEM((rows, width), f32),
            pltpu.VMEM((2, rows, width), bf16),
            pltpu.VMEM((2, rows, width), bf16),
            pltpu.VMEM((fsdp_n, 2, width), f32),
            pltpu.VMEM((2, width), f32),
            pltpu.VMEM((fsdp_n, 2, width), f32),
            pltpu.VMEM((2, width), f32),
            pltpu.VMEM((places, 2, width), f32),
            dma((2,)),
            dma((2,)),
            dma((2, groups)),
            dma((2, groups)),
            dma((2,)),
            dma((2,)),
            dma((2,)),
            dma((2,)),
            dma((2, groups)),
            dma((2, groups)),
            dma((fsdp_n,)),
            dma((fsdp_n,)),
            dma((fsdp_n,)),
            dma((fsdp_n,)),
            dma((places,)),
            dma((places,)),
        ],
        compiler_params=pltpu.CompilerParams(
            collective_id=0, has_side_effects=True, vmem_limit_bytes=48 * 1024 * 1024
        ),
    )(q_raw[0, 0], k_raw[0, 0], value_in[0, 0], cotangent[0, 0], placed, flags)
    start = lax.axis_index("fsdp") * share
    mine = lax.dynamic_slice_in_dim(gain_sums, start, share, 1)
    return (q_out[None, None], k_out[None, None], v_out[None, None], mine[0], mine[1])


def solution(mesh):
    tokens = P("fsdp", "cfg", "seq", None)
    return jax.shard_map(
        on_device,
        mesh=mesh,
        in_specs=(tokens, tokens, tokens, tokens, P("fsdp"), P("fsdp"), P()),
        out_specs=(tokens, tokens, tokens, P("fsdp"), P("fsdp")),
        check_vma=False,
    )
```

```python
import functools
import math

import jax
import jax.numpy as jnp
from jax import lax
from jax.experimental import pallas as pl
from jax.experimental.pallas import tpu as pltpu
from jax.sharding import PartitionSpec as P

HEAD_DIM = 128
TILE = 64
LOW = -1e30
MESH = pl.DeviceIdType.MESH
NT = (((1,), (1,)), ((), ()))
NN = (((1,), (0,)), ((), ()))
TN = (((0,), (0,)), ((), ()))


def dot(a, b, dims):
    return lax.dot_general(a, b, dims, preferred_element_type=jnp.float32)


def fused(
    sizes,
    c_hbm,
    q_hbm,
    k_hbm,
    v_hbm,
    gq_ref,
    gk_ref,
    lists_ref,
    dq_ref,
    dk_ref,
    dv_ref,
    sum_ref,
    q_ref,
    k_ref,
    v_ref,
    c_ref,
    qn,
    kn,
    hq,
    hc,
    mask,
    s_buf,
    p_buf,
    stat,
    stat_in,
    fin,
    fin_in,
    dq_own,
    dq_send,
    dq_in,
    gain,
    gslots,
    gp,
    fslots,
    gp2,
    cslots,
    load_sem,
    hc_send,
    hc_recv,
    hq_send,
    hq_recv,
    st_send,
    st_recv,
    fin_send,
    fin_recv,
    dq_ssem,
    dq_rsem,
    g_send,
    g_recv,
    f_send,
    f_recv,
    x_send,
    x_recv,
):
    seq_n, cfg_n, fsdp_n, heads, group_heads, share = sizes
    rows, width = q_ref.shape
    aligned = share % 128 == 0
    groups = heads // group_heads
    group_width = group_heads * HEAD_DIM
    slab_tiles = rows // TILE
    list_len = lists_ref.shape[0]
    score_scale = 1.0 / math.sqrt(HEAD_DIM)
    z = lax.axis_index("seq")
    c = lax.axis_index("cfg")
    f = lax.axis_index("fsdp")
    place = z * cfg_n + c
    here = (z > 0, z < seq_n - 1)
    there = (z - 1, z + 1)

    loads = [
        pltpu.make_async_copy(src, dst, load_sem.at[i])
        for i, (src, dst) in enumerate(
            ((q_hbm, q_ref), (k_hbm, k_ref), (c_hbm, c_ref), (v_hbm, v_ref))
        )
    ]
    for load in loads:
        load.start()

    fsdp_peers = [lax.rem(f + i, fsdp_n) for i in range(1, fsdp_n)]
    row_peers = [lax.rem(place + i, seq_n * cfg_n) for i in range(1, seq_n * cfg_n)]

    def row_id(peer):
        return {"seq": lax.div(peer, cfg_n), "cfg": lax.rem(peer, cfg_n)}

    barrier = pltpu.get_barrier_semaphore()
    for peer in row_peers:
        pl.semaphore_signal(barrier, inc=1, device_id=row_id(peer), device_id_type=MESH)
    for peer in fsdp_peers:
        pl.semaphore_signal(barrier, inc=1, device_id={"fsdp": peer}, device_id_type=MESH)
    pl.semaphore_wait(barrier, len(fsdp_peers) + len(row_peers))

    def columns(h):
        return pl.ds(pl.multiple_of(h * HEAD_DIM, HEAD_DIM), HEAD_DIM)

    def group_columns(g):
        return pl.ds(pl.multiple_of(g * group_width, HEAD_DIM), group_width)

    def link(arriving, side, src, dst, send, recv, tail, g):
        slot = side if arriving else 1 - side
        return pltpu.make_async_remote_copy(
            src_ref=src,
            dst_ref=dst.at[(slot,) + tail],
            send_sem=send.at[side, g],
            recv_sem=recv.at[slot, g],
            device_id={"seq": there[side]},
            device_id_type=MESH,
        )

    def c_chunk(arriving, side, g):
        cols = group_columns(g)
        return link(
            arriving, side, c_hbm.at[:, cols], hc, hc_send, hc_recv, (slice(None), cols), g
        )

    def q_chunk(arriving, side, g):
        cols = group_columns(g)
        return link(arriving, side, qn.at[:, cols], hq, hq_send, hq_recv, (slice(None), cols), g)

    def stat_chunk(arriving, side, g):
        return link(arriving, side, stat.at[2 * side, g], stat_in, st_send, st_recv, (g,), g)

    def fin_chunk(arriving, side, g):
        return link(arriving, side, fin.at[g], fin_in, fin_send, fin_recv, (g,), g)

    def dq_chunk(arriving, side, g):
        cols = group_columns(g)
        return link(
            arriving,
            side,
            dq_send.at[side, :, cols],
            dq_in,
            dq_ssem,
            dq_rsem,
            (slice(None), cols),
            g,
        )

    def each_side(action):
        for side in range(2):

            @pl.when(here[side])
            def _(side=side):
                action(side)

    ahead = min(2, groups)

    def first_sends(side):
        for g in range(ahead):
            c_chunk(False, side, g).start()

    each_side(first_sends)

    def peer_copy(src, dst, send, recv, target):
        return pltpu.make_async_remote_copy(
            src_ref=src,
            dst_ref=dst,
            send_sem=send,
            recv_sem=recv,
            device_id=target,
            device_id_type=MESH,
        )

    def piece(ref, i):
        if aligned:
            return ref.at[:, pl.ds(pl.multiple_of(i * share, 128), share)]
        return ref

    own_gains = (gq_ref, gk_ref)

    def gain_copy(row, owner, peer):
        target = piece(gain.at[row], owner) if aligned else gslots.at[row, owner]
        return peer_copy(
            own_gains[row], target, g_send.at[row, peer], g_recv.at[row, owner], {"fsdp": peer}
        )

    for peer in fsdp_peers:
        for row in range(2):
            gain_copy(row, f, peer).start()
    for row in range(2):
        if aligned:
            gain[row, :, pl.ds(pl.multiple_of(f * share, 128), share)] = own_gains[row][...]
        else:
            gslots[row, f] = own_gains[row][...]

    for side in range(2):

        @pl.when(jnp.logical_not(here[side]))
        def _(side=side):
            hq[side] = jnp.zeros((rows, width), jnp.bfloat16)
            hc[side] = jnp.zeros((rows, width), jnp.bfloat16)
            dq_in[side] = jnp.zeros((rows, width), jnp.bfloat16)
            fin_in[side] = jnp.zeros((groups, 3 * group_heads, rows), jnp.float32)
            stat_in[side, :, :group_heads] = jnp.full(
                (groups, group_heads, rows), LOW, jnp.float32
            )
            stat_in[side, :, group_heads:] = jnp.zeros(
                (groups, 2 * group_heads, rows), jnp.float32
            )

    zeros = jnp.zeros((rows, HEAD_DIM), jnp.float32)

    def inverse_scale_of(raw_ref):
        def square_step(g, total):
            for j in range(group_heads):
                block = raw_ref[:, columns(g * group_heads + j)].astype(jnp.float32)
                total = total + block * block
            return total

        total = lax.fori_loop(0, groups, square_step, zeros)
        return 1.0 / jnp.sqrt(jnp.sum(total, axis=1, keepdims=True) / width + 1e-06)

    loads[0].wait()
    q_inv = inverse_scale_of(q_ref)
    loads[1].wait()
    k_inv = inverse_scale_of(k_ref)

    for peer in fsdp_peers:
        for row in range(2):
            gain_copy(row, peer, peer).wait()
    if not aligned:
        for row in range(2):
            gains = gslots[row, 0]
            for i in range(1, fsdp_n):
                gains = gains + gslots[row, i]
            gain[row] = gains

    def head_gain(row, h):
        return gain[row, :, columns(h)]

    def normalize(raw_ref, row, inverse, out):
        @pl.loop(0, groups)
        def _(g):
            for j in range(group_heads):
                cols = columns(g * group_heads + j)
                out[:, cols] = (
                    raw_ref[:, cols].astype(jnp.float32)
                    * inverse
                    * head_gain(row, g * group_heads + j)
                ).astype(jnp.bfloat16)

    normalize(q_ref, 0, q_inv, qn)

    def second_sends(side):
        for g in range(ahead):
            q_chunk(False, side, g).start()

    each_side(second_sends)
    normalize(k_ref, 1, k_inv, kn)

    lane_tile = lax.broadcasted_iota(jnp.int32, (1, rows), 1) // TILE

    @pl.loop(0, heads)
    def _(h):
        for slot in range(3):
            slab = jnp.clip(z + (slot - 1), 0, seq_n - 1)
            real = 1 if slot == 1 else here[slot // 2].astype(jnp.int32)
            for key_tile in range(slab_tiles):
                target = z * slab_tiles + key_tile
                line = jnp.zeros((1, rows), jnp.float32)
                for query_tile in range(slab_tiles):
                    hits = 0
                    for i in range(list_len):
                        picked = lists_ref[i, slab * slab_tiles + query_tile, h]
                        hits = hits + (picked == target).astype(jnp.int32)
                    hits = (hits * real).astype(jnp.float32)
                    line = jnp.where(lane_tile == query_tile, hits, line)
                at = slot * slab_tiles + key_tile
                mask[h, at : at + 1] = line

    loads[2].wait()
    loads[3].wait()

    def stats_of(slot, g, j, queries, cots):
        h = g * group_heads + j
        cols = columns(h)
        scores = dot(kn[:, cols], queries, NT) * score_scale
        probs = dot(v_ref[:, cols], cots, NT)
        live = (
            jnp.concatenate(
                [
                    jnp.broadcast_to(
                        mask[h, slot * slab_tiles + t : slot * slab_tiles + t + 1], (TILE, rows)
                    )
                    for t in range(slab_tiles)
                ],
                axis=0,
            )
            > 0.5
        )
        scores = jnp.where(live, scores, LOW)
        top = jnp.max(scores, axis=0, keepdims=True)
        expo = jnp.where(live, jnp.exp(scores - top), 0.0)
        s_buf[slot, h] = scores
        p_buf[slot, h] = probs
        stat[slot, g, j : j + 1] = top
        stat[slot, g, group_heads + j : group_heads + j + 1] = jnp.sum(
            expo, axis=0, keepdims=True
        )
        stat[slot, g, 2 * group_heads + j : 2 * group_heads + j + 1] = jnp.sum(
            expo * probs, axis=0, keepdims=True
        )

    def back_of(slot, g, j, final, queries, cots):
        h = g * group_heads + j
        top = final[j : j + 1]
        inverse = final[group_heads + j : group_heads + j + 1]
        delta = final[2 * group_heads + j : 2 * group_heads + j + 1]
        weights = jnp.exp(s_buf[slot, h] - top) * inverse
        grads = (weights * (p_buf[slot, h] - delta) * score_scale).astype(jnp.bfloat16)
        return (
            dot(grads, kn[:, columns(h)], TN),
            dot(grads, queries, NN),
            dot(weights.astype(jnp.bfloat16), cots, NN),
        )

    def stats_stage(g):
        for j in range(group_heads):
            cols = columns(g * group_heads + j)
            stats_of(1, g, j, qn[:, cols], c_ref[:, cols])

        def arrive(side):
            c_chunk(True, side, g).wait_recv()
            q_chunk(True, side, g).wait_recv()

        each_side(arrive)
        for j in range(group_heads):
            cols = columns(g * group_heads + j)
            for side in range(2):
                stats_of(2 * side, g, j, hq[side, :, cols], hc[side, :, cols])
        each_side(lambda side: stat_chunk(False, side, g).start())

    def merge_stage(g):
        each_side(lambda side: stat_chunk(True, side, g).wait_recv())
        parts = (stat_in[0, g], stat[1, g], stat_in[1, g])
        tops = [part[:group_heads] for part in parts]
        top = jnp.maximum(jnp.maximum(tops[0], tops[1]), tops[2])
        factors = [jnp.exp(part - top) for part in tops]
        total = sum(p[group_heads : 2 * group_heads] * w for p, w in zip(parts, factors))
        weighted = sum(p[2 * group_heads :] * w for p, w in zip(parts, factors))
        inverse = 1.0 / total
        fin[g, :group_heads] = top
        fin[g, group_heads : 2 * group_heads] = inverse
        fin[g, 2 * group_heads :] = weighted * inverse
        each_side(lambda side: fin_chunk(False, side, g).start())

    def back_stage(g):
        each_side(lambda side: fin_chunk(True, side, g).wait_recv())
        finals = (fin_in[0, g], fin[g], fin_in[1, g])
        for j in range(group_heads):
            cols = columns(g * group_heads + j)
            left = back_of(0, g, j, finals[0], hq[0, :, cols], hc[0, :, cols])
            right = back_of(2, g, j, finals[2], hq[1, :, cols], hc[1, :, cols])
            own = back_of(1, g, j, finals[1], qn[:, cols], c_ref[:, cols])
            dq_send[0, :, cols] = left[0].astype(jnp.bfloat16)
            dq_send[1, :, cols] = right[0].astype(jnp.bfloat16)
            dq_own[:, cols] = own[0]
            dk_ref[:, cols] = (left[1] + right[1] + own[1]).astype(jnp.bfloat16)
            dv_ref[:, cols] = (left[2] + right[2] + own[2]).astype(jnp.bfloat16)
        each_side(lambda side: dq_chunk(False, side, g).start())

    @pl.loop(0, groups + 2)
    def _(i):
        @pl.when(i < groups)
        def _():
            stats_stage(i)

        @pl.when(jnp.logical_and(i >= 1, i <= groups))
        def _():
            merge_stage(i - 1)

        @pl.when(i >= 2)
        def _():
            back_stage(i - 2)

        @pl.when(i + ahead < groups)
        def _():
            def more(side):
                c_chunk(False, side, i + ahead).start()
                q_chunk(False, side, i + ahead).start()

            each_side(more)

    def inner_step(row, raw_ref, inverse, g, inner, grad_of):
        for j in range(group_heads):
            h = g * group_heads + j
            cols = columns(h)
            raw = raw_ref[:, cols].astype(jnp.float32)
            grad = grad_of(cols)
            gp[row, :, cols] = jnp.sum(grad * (raw * inverse), axis=0, keepdims=True)
            inner = inner + raw * (grad * head_gain(row, h))
        return inner

    def finish(row, raw_ref, out_ref, inverse, inner):
        inner = jnp.sum(inner, axis=1, keepdims=True)
        ratio = inner / width * (inverse * inverse * inverse)

        @pl.loop(0, groups)
        def _(g):
            for j in range(group_heads):
                h = g * group_heads + j
                cols = columns(h)
                raw = raw_ref[:, cols].astype(jnp.float32)
                grad = out_ref[:, cols].astype(jnp.float32)
                out_ref[:, cols] = (
                    grad * head_gain(row, h) * inverse - raw * ratio
                ).astype(jnp.bfloat16)

    def fold_copy(row, owner, peer, part):
        return peer_copy(
            piece(gp.at[row], part),
            fslots.at[row, owner],
            f_send.at[row, peer],
            f_recv.at[row, owner],
            {"fsdp": peer},
        )

    def spread_copy(row, owner, peer):
        return peer_copy(
            gp2.at[row],
            cslots.at[row, owner],
            x_send.at[row, peer],
            x_recv.at[row, owner],
            row_id(peer),
        )

    def fold_start(row):
        for peer in fsdp_peers:
            fold_copy(row, f, peer, peer).start()
        fslots[row, f] = piece(gp.at[row], f)[...]

    def spread_start(row):
        for peer in fsdp_peers:
            fold_copy(row, peer, peer, peer).wait()
        part = fslots[row, 0]
        for i in range(1, fsdp_n):
            part = part + fslots[row, i]
        gp2[row] = part
        for peer in row_peers:
            spread_copy(row, place, peer).start()
        cslots[row, place] = part

    def spread_end(row):
        for peer in row_peers:
            spread_copy(row, peer, peer).wait()
        part = cslots[row, 0]
        for i in range(1, seq_n * cfg_n):
            part = part + cslots[row, i]
        sum_ref[row] = part / (2.0 * fsdp_n)

    inner = lax.fori_loop(
        0,
        groups,
        lambda g, inner: inner_step(
            1, k_ref, k_inv, g, inner, lambda cols: dk_ref[:, cols].astype(jnp.float32)
        ),
        zeros,
    )
    fold_start(1)
    finish(1, k_ref, dk_ref, k_inv, inner)
    spread_start(1)

    def join_step(g, inner):
        each_side(lambda side: dq_chunk(True, side, g).wait_recv())

        def joined(cols):
            total = (
                dq_own[:, cols]
                + dq_in[0, :, cols].astype(jnp.float32)
                + dq_in[1, :, cols].astype(jnp.float32)
            ).astype(jnp.bfloat16)
            dq_ref[:, cols] = total
            return total.astype(jnp.float32)

        return inner_step(0, q_ref, q_inv, g, inner, joined)

    inner = lax.fori_loop(0, groups, join_step, zeros)
    fold_start(0)
    finish(0, q_ref, dq_ref, q_inv, inner)
    spread_start(0)
    spread_end(1)

    def drain(side):
        @pl.loop(0, groups)
        def _(g):
            for chunk in (c_chunk, q_chunk, stat_chunk, fin_chunk, dq_chunk):
                chunk(False, side, g).wait_send()

    each_side(drain)
    spread_end(0)


def on_device(q_raw, k_raw, value_in, cotangent, q_gain, k_gain, tile_lists):
    seq_n, cfg_n, fsdp_n = (lax.axis_size(name) for name in ("seq", "cfg", "fsdp"))
    rows, width = q_raw.shape[2:]
    heads = width // HEAD_DIM
    share = q_gain.shape[0]
    group_heads = next(n for n in (4, 3, 2, 1) if heads % n == 0)
    groups = heads // group_heads
    aligned = share % 128 == 0
    start = lax.axis_index("fsdp") * share

    def own_gain(gain):
        if aligned:
            return gain[None]
        owner = lax.broadcasted_iota(jnp.int32, (1, width), 1) // share
        return jnp.where(owner == lax.axis_index("fsdp"), jnp.tile(gain, fsdp_n)[None], 0.0)

    bf16, f32 = jnp.bfloat16, jnp.float32
    dma = pltpu.SemaphoreType.DMA
    places = seq_n * cfg_n
    piece = share if aligned else width
    vmem = pl.BlockSpec(memory_space=pltpu.VMEM)
    hbm = pl.BlockSpec(memory_space=pltpu.HBM)
    grad = jax.ShapeDtypeStruct((rows, width), bf16)
    slab = pltpu.VMEM((rows, width), bf16)
    slabs = pltpu.VMEM((2, rows, width), bf16)
    lines = 3 * group_heads
    q_out, k_out, v_out, gain_sums = pl.pallas_call(
        functools.partial(fused, (seq_n, cfg_n, fsdp_n, heads, group_heads, share)),
        out_shape=(grad, grad, grad, jax.ShapeDtypeStruct((2, 1, piece), f32)),
        in_specs=[hbm] * 4 + [vmem] * 2 + [pl.BlockSpec(memory_space=pltpu.SMEM)],
        out_specs=(vmem,) * 4,
        scratch_shapes=[
            slab,
            slab,
            slab,
            slab,
            slab,
            slab,
            slabs,
            slabs,
            pltpu.VMEM((heads, 3 * (rows // TILE), rows), f32),
            pltpu.VMEM((3, heads, rows, rows), f32),
            pltpu.VMEM((3, heads, rows, rows), f32),
            pltpu.VMEM((3, groups, lines, rows), f32),
            pltpu.VMEM((2, groups, lines, rows), f32),
            pltpu.VMEM((groups, lines, rows), f32),
            pltpu.VMEM((2, groups, lines, rows), f32),
            pltpu.VMEM((rows, width), f32),
            slabs,
            slabs,
            pltpu.VMEM((2, 1, width), f32),
            pltpu.VMEM((2, 1, 1, 128) if aligned else (2, fsdp_n, 1, width), f32),
            pltpu.VMEM((2, 1, width), f32),
            pltpu.VMEM((2, fsdp_n, 1, piece), f32),
            pltpu.VMEM((2, 1, piece), f32),
            pltpu.VMEM((2, places, 1, piece), f32),
            dma((4,)),
        ]
        + [dma((2, groups))] * 10
        + [dma((2, fsdp_n))] * 4
        + [dma((2, places))] * 2,
        compiler_params=pltpu.CompilerParams(
            collective_id=0, has_side_effects=True, vmem_limit_bytes=48 * 1024 * 1024
        ),
    )(
        cotangent[0, 0],
        q_raw[0, 0],
        k_raw[0, 0],
        value_in[0, 0],
        own_gain(q_gain),
        own_gain(k_gain),
        tile_lists.transpose(2, 1, 0),
    )
    sums = gain_sums[:, 0]
    if not aligned:
        sums = lax.dynamic_slice_in_dim(sums, start, share, 1)
    return (q_out[None, None], k_out[None, None], v_out[None, None], sums[0], sums[1])


def solution(mesh):
    tokens = P("fsdp", "cfg", "seq", None)
    return jax.shard_map(
        on_device,
        mesh=mesh,
        in_specs=(tokens, tokens, tokens, tokens, P("fsdp"), P("fsdp"), P()),
        out_specs=(tokens, tokens, tokens, P("fsdp"), P("fsdp")),
        check_vma=False,
    )
```

```python
import functools
import math

import jax
import jax.numpy as jnp
from jax import lax
from jax.experimental import pallas as pl
from jax.experimental.pallas import tpu as pltpu
from jax.sharding import PartitionSpec as P

HEAD_DIM = 128
TILE = 64
LOW = -1e30
MESH = pl.DeviceIdType.MESH
NT = (((1,), (1,)), ((), ()))
NN = (((1,), (0,)), ((), ()))
TN = (((0,), (0,)), ((), ()))


def dot(a, b, dims):
    return lax.dot_general(a, b, dims, preferred_element_type=jnp.float32)


def fused(
    sizes,
    c_hbm,
    q_hbm,
    k_hbm,
    v_hbm,
    gq_ref,
    gk_ref,
    lists_ref,
    dq_out,
    dk_out,
    dv_out,
    sum_ref,
    dq_ref,
    dk_ref,
    dv_ref,
    q_ref,
    k_ref,
    v_ref,
    c_ref,
    qn,
    kn,
    hq,
    hc,
    mask,
    s_buf,
    p_buf,
    stat,
    stat_in,
    fin,
    fin_in,
    dq_own,
    dq_send,
    dq_in,
    gain,
    gslots,
    gp,
    fslots,
    gp2,
    cslots,
    load_sem,
    out_sem,
    hc_send,
    hc_recv,
    hq_send,
    hq_recv,
    st_send,
    st_recv,
    fin_send,
    fin_recv,
    dq_ssem,
    dq_rsem,
    g_send,
    g_recv,
    f_send,
    f_recv,
    x_send,
    x_recv,
):
    seq_n, cfg_n, fsdp_n, heads, group_heads, share = sizes
    rows, width = q_ref.shape
    aligned = share % 128 == 0
    groups = heads // group_heads
    group_width = group_heads * HEAD_DIM
    slab_tiles = rows // TILE
    list_len = lists_ref.shape[0]
    score_scale = 1.0 / math.sqrt(HEAD_DIM)
    z = lax.axis_index("seq")
    c = lax.axis_index("cfg")
    f = lax.axis_index("fsdp")
    place = z * cfg_n + c
    here = (z > 0, z < seq_n - 1)
    there = (z - 1, z + 1)

    loads = [
        pltpu.make_async_copy(src, dst, load_sem.at[i])
        for i, (src, dst) in enumerate(
            ((q_hbm, q_ref), (k_hbm, k_ref), (c_hbm, c_ref), (v_hbm, v_ref))
        )
    ]
    for load in loads:
        load.start()

    fsdp_peers = [lax.rem(f + i, fsdp_n) for i in range(1, fsdp_n)]
    row_peers = [lax.rem(place + i, seq_n * cfg_n) for i in range(1, seq_n * cfg_n)]

    def row_id(peer):
        return {"seq": lax.div(peer, cfg_n), "cfg": lax.rem(peer, cfg_n)}

    barrier = pltpu.get_barrier_semaphore()
    for peer in row_peers:
        pl.semaphore_signal(barrier, inc=1, device_id=row_id(peer), device_id_type=MESH)
    for peer in fsdp_peers:
        pl.semaphore_signal(barrier, inc=1, device_id={"fsdp": peer}, device_id_type=MESH)
    pl.semaphore_wait(barrier, len(fsdp_peers) + len(row_peers))

    def columns(h):
        return pl.ds(pl.multiple_of(h * HEAD_DIM, HEAD_DIM), HEAD_DIM)

    def group_columns(g):
        return pl.ds(pl.multiple_of(g * group_width, HEAD_DIM), group_width)

    def link(arriving, side, src, dst, send, recv, tail, g):
        slot = side if arriving else 1 - side
        return pltpu.make_async_remote_copy(
            src_ref=src,
            dst_ref=dst.at[(slot,) + tail],
            send_sem=send.at[side, g],
            recv_sem=recv.at[slot, g],
            device_id={"seq": there[side]},
            device_id_type=MESH,
        )

    def c_chunk(arriving, side, g):
        cols = group_columns(g)
        return link(
            arriving, side, c_hbm.at[:, cols], hc, hc_send, hc_recv, (slice(None), cols), g
        )

    def q_chunk(arriving, side, g):
        cols = group_columns(g)
        return link(arriving, side, qn.at[:, cols], hq, hq_send, hq_recv, (slice(None), cols), g)

    def stat_chunk(arriving, side, g):
        return link(arriving, side, stat.at[2 * side, g], stat_in, st_send, st_recv, (g,), g)

    def fin_chunk(arriving, side, g):
        return link(arriving, side, fin.at[g], fin_in, fin_send, fin_recv, (g,), g)

    def dq_chunk(arriving, side, g):
        cols = group_columns(g)
        return link(
            arriving,
            side,
            dq_send.at[side, :, cols],
            dq_in,
            dq_ssem,
            dq_rsem,
            (slice(None), cols),
            g,
        )

    def each_side(action):
        for side in range(2):

            @pl.when(here[side])
            def _(side=side):
                action(side)

    ahead = min(2, groups)

    def first_sends(side):
        for g in range(ahead):
            c_chunk(False, side, g).start()

    each_side(first_sends)

    def peer_copy(src, dst, send, recv, target):
        return pltpu.make_async_remote_copy(
            src_ref=src,
            dst_ref=dst,
            send_sem=send,
            recv_sem=recv,
            device_id=target,
            device_id_type=MESH,
        )

    def piece(ref, i):
        if aligned:
            return ref.at[:, pl.ds(pl.multiple_of(i * share, 128), share)]
        return ref

    own_gains = (gq_ref, gk_ref)

    def gain_copy(row, owner, peer):
        target = piece(gain.at[row], owner) if aligned else gslots.at[row, owner]
        return peer_copy(
            own_gains[row], target, g_send.at[row, peer], g_recv.at[row, owner], {"fsdp": peer}
        )

    for peer in fsdp_peers:
        for row in range(2):
            gain_copy(row, f, peer).start()
    for row in range(2):
        if aligned:
            gain[row, :, pl.ds(pl.multiple_of(f * share, 128), share)] = own_gains[row][...]
        else:
            gslots[row, f] = own_gains[row][...]

    for side in range(2):

        @pl.when(jnp.logical_not(here[side]))
        def _(side=side):
            hq[side] = jnp.zeros((rows, width), jnp.bfloat16)
            hc[side] = jnp.zeros((rows, width), jnp.bfloat16)
            dq_in[side] = jnp.zeros((rows, width), jnp.bfloat16)
            fin_in[side] = jnp.zeros((groups, 3 * group_heads, rows), jnp.float32)
            stat_in[side, :, :group_heads] = jnp.full(
                (groups, group_heads, rows), LOW, jnp.float32
            )
            stat_in[side, :, group_heads:] = jnp.zeros(
                (groups, 2 * group_heads, rows), jnp.float32
            )

    zeros = jnp.zeros((rows, HEAD_DIM), jnp.float32)

    def inverse_scale_of(raw_ref):
        def square_step(g, total):
            for j in range(group_heads):
                block = raw_ref[:, columns(g * group_heads + j)].astype(jnp.float32)
                total = total + block * block
            return total

        total = lax.fori_loop(0, groups, square_step, zeros)
        return 1.0 / jnp.sqrt(jnp.sum(total, axis=1, keepdims=True) / width + 1e-06)

    loads[0].wait()
    q_inv = inverse_scale_of(q_ref)
    loads[1].wait()
    k_inv = inverse_scale_of(k_ref)

    for peer in fsdp_peers:
        for row in range(2):
            gain_copy(row, peer, peer).wait()
    if not aligned:
        for row in range(2):
            gains = gslots[row, 0]
            for i in range(1, fsdp_n):
                gains = gains + gslots[row, i]
            gain[row] = gains

    def head_gain(row, h):
        return gain[row, :, columns(h)]

    def normalize(raw_ref, row, inverse, out):
        @pl.loop(0, groups)
        def _(g):
            for j in range(group_heads):
                cols = columns(g * group_heads + j)
                out[:, cols] = (
                    raw_ref[:, cols].astype(jnp.float32)
                    * inverse
                    * head_gain(row, g * group_heads + j)
                ).astype(jnp.bfloat16)

    normalize(q_ref, 0, q_inv, qn)

    def second_sends(side):
        for g in range(ahead):
            q_chunk(False, side, g).start()

    each_side(second_sends)
    normalize(k_ref, 1, k_inv, kn)

    lane_tile = lax.broadcasted_iota(jnp.int32, (1, rows), 1) // TILE

    @pl.loop(0, heads)
    def _(h):
        for slot in range(3):
            slab = jnp.clip(z + (slot - 1), 0, seq_n - 1)
            real = 1 if slot == 1 else here[slot // 2].astype(jnp.int32)
            for key_tile in range(slab_tiles):
                target = z * slab_tiles + key_tile
                line = jnp.zeros((1, rows), jnp.float32)
                for query_tile in range(slab_tiles):
                    hits = 0
                    for i in range(list_len):
                        picked = lists_ref[i, slab * slab_tiles + query_tile, h]
                        hits = hits + (picked == target).astype(jnp.int32)
                    hits = (hits * real).astype(jnp.float32)
                    line = jnp.where(lane_tile == query_tile, hits, line)
                at = slot * slab_tiles + key_tile
                mask[h, at : at + 1] = line

    loads[2].wait()
    loads[3].wait()

    def stats_of(slot, g, j, queries, cots):
        h = g * group_heads + j
        cols = columns(h)
        scores = dot(kn[:, cols], queries, NT) * score_scale
        probs = dot(v_ref[:, cols], cots, NT)
        live = (
            jnp.concatenate(
                [
                    jnp.broadcast_to(
                        mask[h, slot * slab_tiles + t : slot * slab_tiles + t + 1], (TILE, rows)
                    )
                    for t in range(slab_tiles)
                ],
                axis=0,
            )
            > 0.5
        )
        scores = jnp.where(live, scores, LOW)
        top = jnp.max(scores, axis=0, keepdims=True)
        expo = jnp.where(live, jnp.exp(scores - top), 0.0)
        s_buf[slot, h] = scores
        p_buf[slot, h] = probs
        stat[slot, g, j : j + 1] = top
        stat[slot, g, group_heads + j : group_heads + j + 1] = jnp.sum(
            expo, axis=0, keepdims=True
        )
        stat[slot, g, 2 * group_heads + j : 2 * group_heads + j + 1] = jnp.sum(
            expo * probs, axis=0, keepdims=True
        )

    def back_of(slot, g, j, final, queries, cots):
        h = g * group_heads + j
        top = final[j : j + 1]
        inverse = final[group_heads + j : group_heads + j + 1]
        delta = final[2 * group_heads + j : 2 * group_heads + j + 1]
        weights = jnp.exp(s_buf[slot, h] - top) * inverse
        grads = (weights * (p_buf[slot, h] - delta) * score_scale).astype(jnp.bfloat16)
        return (
            dot(grads, kn[:, columns(h)], TN),
            dot(grads, queries, NN),
            dot(weights.astype(jnp.bfloat16), cots, NN),
        )

    def stats_stage(g):
        for j in range(group_heads):
            cols = columns(g * group_heads + j)
            stats_of(1, g, j, qn[:, cols], c_ref[:, cols])

        def arrive(side):
            c_chunk(True, side, g).wait_recv()
            q_chunk(True, side, g).wait_recv()

        each_side(arrive)
        for j in range(group_heads):
            cols = columns(g * group_heads + j)
            for side in range(2):
                stats_of(2 * side, g, j, hq[side, :, cols], hc[side, :, cols])
        each_side(lambda side: stat_chunk(False, side, g).start())

    def merge_stage(g):
        each_side(lambda side: stat_chunk(True, side, g).wait_recv())
        parts = (stat_in[0, g], stat[1, g], stat_in[1, g])
        tops = [part[:group_heads] for part in parts]
        top = jnp.maximum(jnp.maximum(tops[0], tops[1]), tops[2])
        factors = [jnp.exp(part - top) for part in tops]
        total = sum(p[group_heads : 2 * group_heads] * w for p, w in zip(parts, factors))
        weighted = sum(p[2 * group_heads :] * w for p, w in zip(parts, factors))
        inverse = 1.0 / total
        fin[g, :group_heads] = top
        fin[g, group_heads : 2 * group_heads] = inverse
        fin[g, 2 * group_heads :] = weighted * inverse
        each_side(lambda side: fin_chunk(False, side, g).start())

    def back_stage(g):
        each_side(lambda side: fin_chunk(True, side, g).wait_recv())
        finals = (fin_in[0, g], fin[g], fin_in[1, g])
        for j in range(group_heads):
            cols = columns(g * group_heads + j)
            left = back_of(0, g, j, finals[0], hq[0, :, cols], hc[0, :, cols])
            right = back_of(2, g, j, finals[2], hq[1, :, cols], hc[1, :, cols])
            own = back_of(1, g, j, finals[1], qn[:, cols], c_ref[:, cols])
            dq_send[0, :, cols] = left[0].astype(jnp.bfloat16)
            dq_send[1, :, cols] = right[0].astype(jnp.bfloat16)
            dq_own[:, cols] = own[0]
            dk_ref[:, cols] = (left[1] + right[1] + own[1]).astype(jnp.bfloat16)
            dv_ref[:, cols] = (left[2] + right[2] + own[2]).astype(jnp.bfloat16)
            h = g * group_heads + j
            q_terms = (
                left[0] * hq[0, :, cols].astype(jnp.float32)
                + right[0] * hq[1, :, cols].astype(jnp.float32)
                + own[0] * qn[:, cols].astype(jnp.float32)
            )
            k_terms = dk_ref[:, cols].astype(jnp.float32) * kn[:, cols].astype(jnp.float32)
            gp[0, :, cols] = jnp.sum(q_terms, axis=0, keepdims=True) / head_gain(0, h)
            gp[1, :, cols] = jnp.sum(k_terms, axis=0, keepdims=True) / head_gain(1, h)
        each_side(lambda side: dq_chunk(False, side, g).start())

    @pl.loop(0, groups + 2)
    def _(i):
        @pl.when(i < groups)
        def _():
            stats_stage(i)

        @pl.when(jnp.logical_and(i >= 1, i <= groups))
        def _():
            merge_stage(i - 1)

        @pl.when(i >= 2)
        def _():
            back_stage(i - 2)

        @pl.when(i + ahead < groups)
        def _():
            def more(side):
                c_chunk(False, side, i + ahead).start()
                q_chunk(False, side, i + ahead).start()

            each_side(more)

    def inner_step(row, raw_ref, inverse, g, inner, grad_of):
        for j in range(group_heads):
            h = g * group_heads + j
            cols = columns(h)
            raw = raw_ref[:, cols].astype(jnp.float32)
            grad = grad_of(cols)
            inner = inner + raw * (grad * head_gain(row, h))
        return inner

    def finish(row, raw_ref, out_ref, inverse, inner):
        inner = jnp.sum(inner, axis=1, keepdims=True)
        ratio = inner / width * (inverse * inverse * inverse)

        @pl.loop(0, groups)
        def _(g):
            for j in range(group_heads):
                h = g * group_heads + j
                cols = columns(h)
                raw = raw_ref[:, cols].astype(jnp.float32)
                grad = out_ref[:, cols].astype(jnp.float32)
                out_ref[:, cols] = (
                    grad * head_gain(row, h) * inverse - raw * ratio
                ).astype(jnp.bfloat16)

    def gain_piece(i):
        if aligned:
            return gp.at[:, :, pl.ds(pl.multiple_of(i * share, 128), share)]
        return gp

    def fold_copy(owner, peer):
        return peer_copy(
            gain_piece(peer), fslots.at[owner], f_send.at[peer], f_recv.at[owner], {"fsdp": peer}
        )

    def spread_copy(owner, peer):
        return peer_copy(
            gp2, cslots.at[owner], x_send.at[peer], x_recv.at[owner], row_id(peer)
        )

    outs = [
        pltpu.make_async_copy(src, dst, out_sem.at[i])
        for i, (src, dst) in enumerate(((dq_ref, dq_out), (dk_ref, dk_out), (dv_ref, dv_out)))
    ]
    for peer in fsdp_peers:
        fold_copy(f, peer).start()
    fslots[f] = gain_piece(f)[...]
    outs[2].start()

    inner = lax.fori_loop(
        0,
        groups,
        lambda g, inner: inner_step(
            1, k_ref, k_inv, g, inner, lambda cols: dk_ref[:, cols].astype(jnp.float32)
        ),
        zeros,
    )

    for peer in fsdp_peers:
        fold_copy(peer, peer).wait()
    part = fslots[0]
    for i in range(1, fsdp_n):
        part = part + fslots[i]
    gp2[...] = part
    for peer in row_peers:
        spread_copy(place, peer).start()
    cslots[place] = part

    finish(1, k_ref, dk_ref, k_inv, inner)
    outs[1].start()

    def join_step(g, inner):
        each_side(lambda side: dq_chunk(True, side, g).wait_recv())

        def joined(cols):
            total = (
                dq_own[:, cols]
                + dq_in[0, :, cols].astype(jnp.float32)
                + dq_in[1, :, cols].astype(jnp.float32)
            ).astype(jnp.bfloat16)
            dq_ref[:, cols] = total
            return total.astype(jnp.float32)

        return inner_step(0, q_ref, q_inv, g, inner, joined)

    inner = lax.fori_loop(0, groups, join_step, zeros)
    finish(0, q_ref, dq_ref, q_inv, inner)
    outs[0].start()

    for peer in row_peers:
        spread_copy(peer, peer).wait()
    part = cslots[0]
    for i in range(1, seq_n * cfg_n):
        part = part + cslots[i]
    sum_ref[...] = part / (2.0 * fsdp_n)

    def drain(side):
        @pl.loop(0, groups)
        def _(g):
            for chunk in (c_chunk, q_chunk, stat_chunk, fin_chunk, dq_chunk):
                chunk(False, side, g).wait_send()

    each_side(drain)
    for out in outs:
        out.wait()


def move(*refs):
    count = len(refs) // 3
    sources, targets, buffers = (refs[i * count : (i + 1) * count] for i in range(3))

    def with_sems(in_sem, out_sem):
        reads = [
            pltpu.make_async_copy(src, buf, in_sem.at[i])
            for i, (src, buf) in enumerate(zip(sources, buffers))
        ]
        writes = [
            pltpu.make_async_copy(buf, dst, out_sem.at[i])
            for i, (buf, dst) in enumerate(zip(buffers, targets))
        ]
        for read in reads:
            read.start()
        for read, write in zip(reads, writes):
            read.wait()
            write.start()
        for write in writes:
            write.wait()

    dma = pltpu.SemaphoreType.DMA((count,))
    pl.run_scoped(with_sems, dma, dma)


def on_device(q_raw, k_raw, value_in, cotangent, q_gain, k_gain, tile_lists):
    seq_n, cfg_n, fsdp_n = (lax.axis_size(name) for name in ("seq", "cfg", "fsdp"))
    rows, width = q_raw.shape[2:]
    heads = width // HEAD_DIM
    share = q_gain.shape[0]
    group_heads = next(n for n in (5, 4, 3, 2, 1) if heads % n == 0)
    groups = heads // group_heads
    aligned = share % 128 == 0
    start = lax.axis_index("fsdp") * share

    def own_gain(gain):
        if aligned:
            return gain[None]
        owner = lax.broadcasted_iota(jnp.int32, (1, width), 1) // share
        return jnp.where(owner == lax.axis_index("fsdp"), jnp.tile(gain, fsdp_n)[None], 0.0)

    bf16, f32 = jnp.bfloat16, jnp.float32
    dma = pltpu.SemaphoreType.DMA
    places = seq_n * cfg_n
    piece = share if aligned else width
    vmem = pl.BlockSpec(memory_space=pltpu.VMEM)
    hbm = pl.BlockSpec(memory_space=pltpu.HBM)
    grad = jax.ShapeDtypeStruct((rows, width), bf16)
    slab = pltpu.VMEM((rows, width), bf16)
    slabs = pltpu.VMEM((2, rows, width), bf16)
    lines = 3 * group_heads
    q_out, k_out, v_out, gain_sums = pl.pallas_call(
        functools.partial(fused, (seq_n, cfg_n, fsdp_n, heads, group_heads, share)),
        out_shape=(grad, grad, grad, jax.ShapeDtypeStruct((2, 1, piece), f32)),
        in_specs=[hbm] * 4 + [vmem] * 2 + [pl.BlockSpec(memory_space=pltpu.SMEM)],
        out_specs=(hbm,) * 3 + (vmem,),
        scratch_shapes=[
            slab,
            slab,
            slab,
            slab,
            slab,
            slab,
            slab,
            slab,
            slab,
            slabs,
            slabs,
            pltpu.VMEM((heads, 3 * (rows // TILE), rows), f32),
            pltpu.VMEM((3, heads, rows, rows), f32),
            pltpu.VMEM((3, heads, rows, rows), f32),
            pltpu.VMEM((3, groups, lines, rows), f32),
            pltpu.VMEM((2, groups, lines, rows), f32),
            pltpu.VMEM((groups, lines, rows), f32),
            pltpu.VMEM((2, groups, lines, rows), f32),
            pltpu.VMEM((rows, width), f32),
            slabs,
            slabs,
            pltpu.VMEM((2, 1, width), f32),
            pltpu.VMEM((2, 1, 1, 128) if aligned else (2, fsdp_n, 1, width), f32),
            pltpu.VMEM((2, 1, width), f32),
            pltpu.VMEM((fsdp_n, 2, 1, piece), f32),
            pltpu.VMEM((2, 1, piece), f32),
            pltpu.VMEM((places, 2, 1, piece), f32),
            dma((4,)),
            dma((3,)),
        ]
        + [dma((2, groups))] * 10
        + [dma((2, fsdp_n))] * 2
        + [dma((fsdp_n,))] * 2
        + [dma((places,))] * 2,
        compiler_params=pltpu.CompilerParams(
            collective_id=0, has_side_effects=True, vmem_limit_bytes=62 * 1024 * 1024
        ),
    )(
        cotangent[0, 0],
        q_raw[0, 0],
        k_raw[0, 0],
        value_in[0, 0],
        own_gain(q_gain),
        own_gain(k_gain),
        tile_lists.transpose(2, 1, 0),
    )
    q_out, k_out, v_out = pl.pallas_call(
        move,
        out_shape=(grad,) * 3,
        in_specs=[hbm] * 3,
        out_specs=(hbm,) * 3,
        scratch_shapes=[slab] * 3,
    )(q_out, k_out, v_out)
    sums = gain_sums[:, 0]
    if not aligned:
        sums = lax.dynamic_slice_in_dim(sums, start, share, 1)
    return (q_out[None, None], k_out[None, None], v_out[None, None], sums[0], sums[1])


def solution(mesh):
    tokens = P("fsdp", "cfg", "seq", None)
    return jax.shard_map(
        on_device,
        mesh=mesh,
        in_specs=(tokens, tokens, tokens, tokens, P("fsdp"), P("fsdp"), P()),
        out_specs=(tokens, tokens, tokens, P("fsdp"), P("fsdp")),
        check_vma=False,
    )
```

```python
import functools
import math

import jax
import jax.numpy as jnp
from jax import lax
from jax.experimental import pallas as pl
from jax.experimental.pallas import tpu as pltpu
from jax.sharding import PartitionSpec as P

HEAD_DIM = 128
TILE = 64
LOW = -1e30
MESH = pl.DeviceIdType.MESH
NT = (((1,), (1,)), ((), ()))
NN = (((1,), (0,)), ((), ()))
TN = (((0,), (0,)), ((), ()))


def dot(a, b, dims):
    return lax.dot_general(a, b, dims, preferred_element_type=jnp.float32)


def fused(
    sizes,
    c_hbm,
    q_hbm,
    k_hbm,
    v_hbm,
    gq_ref,
    gk_ref,
    lists_ref,
    dq_out,
    dk_out,
    dv_out,
    sum_ref,
    dq_ref,
    dk_ref,
    dv_ref,
    q_ref,
    k_ref,
    v_ref,
    c_ref,
    qn,
    kn,
    hq,
    hc,
    mask,
    s_buf,
    p_buf,
    stat,
    stat_in,
    fin,
    fin_in,
    dq_own,
    dq_send,
    dq_in,
    gain,
    gslots,
    gp,
    fslots,
    gp2,
    cslots,
    load_sem,
    out_sem,
    hc_send,
    hc_recv,
    hq_send,
    hq_recv,
    st_send,
    st_recv,
    fin_send,
    fin_recv,
    dq_ssem,
    dq_rsem,
    g_send,
    g_recv,
    f_send,
    f_recv,
    x_send,
    x_recv,
):
    seq_n, cfg_n, fsdp_n, heads, group_heads, share = sizes
    rows, width = q_ref.shape
    aligned = share % 128 == 0
    groups = heads // group_heads
    group_width = group_heads * HEAD_DIM
    slab_tiles = rows // TILE
    list_len = lists_ref.shape[0]
    score_scale = 1.0 / math.sqrt(HEAD_DIM)
    z = lax.axis_index("seq")
    c = lax.axis_index("cfg")
    f = lax.axis_index("fsdp")
    place = z * cfg_n + c
    here = (z > 0, z < seq_n - 1)
    there = (z - 1, z + 1)

    loads = [
        pltpu.make_async_copy(src, dst, load_sem.at[i])
        for i, (src, dst) in enumerate(
            ((q_hbm, q_ref), (k_hbm, k_ref), (c_hbm, c_ref), (v_hbm, v_ref))
        )
    ]
    for load in loads:
        load.start()

    fsdp_peers = [lax.rem(f + i, fsdp_n) for i in range(1, fsdp_n)]
    row_peers = [lax.rem(place + i, seq_n * cfg_n) for i in range(1, seq_n * cfg_n)]

    def row_id(peer):
        return {"seq": lax.div(peer, cfg_n), "cfg": lax.rem(peer, cfg_n)}

    barrier = pltpu.get_barrier_semaphore()
    for peer in row_peers:
        pl.semaphore_signal(barrier, inc=1, device_id=row_id(peer), device_id_type=MESH)
    for peer in fsdp_peers:
        pl.semaphore_signal(barrier, inc=1, device_id={"fsdp": peer}, device_id_type=MESH)
    pl.semaphore_wait(barrier, len(fsdp_peers) + len(row_peers))

    def columns(h):
        return pl.ds(pl.multiple_of(h * HEAD_DIM, HEAD_DIM), HEAD_DIM)

    def group_columns(g):
        return pl.ds(pl.multiple_of(g * group_width, HEAD_DIM), group_width)

    def link(arriving, side, src, dst, send, recv, tail, g):
        slot = side if arriving else 1 - side
        return pltpu.make_async_remote_copy(
            src_ref=src,
            dst_ref=dst.at[(slot,) + tail],
            send_sem=send.at[side, g],
            recv_sem=recv.at[slot, g],
            device_id={"seq": there[side]},
            device_id_type=MESH,
        )

    def c_chunk(arriving, side, g):
        cols = group_columns(g)
        return link(
            arriving, side, c_hbm.at[:, cols], hc, hc_send, hc_recv, (slice(None), cols), g
        )

    def q_chunk(arriving, side, g):
        cols = group_columns(g)
        return link(arriving, side, qn.at[:, cols], hq, hq_send, hq_recv, (slice(None), cols), g)

    def stat_chunk(arriving, side, g):
        return link(arriving, side, stat.at[2 * side, g], stat_in, st_send, st_recv, (g,), g)

    def fin_chunk(arriving, side, g):
        return link(arriving, side, fin.at[g], fin_in, fin_send, fin_recv, (g,), g)

    def dq_chunk(arriving, side, g):
        cols = group_columns(g)
        return link(
            arriving,
            side,
            dq_send.at[side, :, cols],
            dq_in,
            dq_ssem,
            dq_rsem,
            (slice(None), cols),
            g,
        )

    def each_side(action):
        for side in range(2):

            @pl.when(here[side])
            def _(side=side):
                action(side)

    ahead = min(2, groups)

    def first_sends(side):
        for g in range(ahead):
            c_chunk(False, side, g).start()

    each_side(first_sends)

    def peer_copy(src, dst, send, recv, target):
        return pltpu.make_async_remote_copy(
            src_ref=src,
            dst_ref=dst,
            send_sem=send,
            recv_sem=recv,
            device_id=target,
            device_id_type=MESH,
        )

    def piece(ref, i):
        if aligned:
            return ref.at[:, pl.ds(pl.multiple_of(i * share, 128), share)]
        return ref

    own_gains = (gq_ref, gk_ref)

    def gain_copy(row, owner, peer):
        target = piece(gain.at[row], owner) if aligned else gslots.at[row, owner]
        return peer_copy(
            own_gains[row], target, g_send.at[row, peer], g_recv.at[row, owner], {"fsdp": peer}
        )

    for peer in fsdp_peers:
        for row in range(2):
            gain_copy(row, f, peer).start()
    for row in range(2):
        if aligned:
            gain[row, :, pl.ds(pl.multiple_of(f * share, 128), share)] = own_gains[row][...]
        else:
            gslots[row, f] = own_gains[row][...]

    for side in range(2):

        @pl.when(jnp.logical_not(here[side]))
        def _(side=side):
            hq[side] = jnp.zeros((rows, width), jnp.bfloat16)
            hc[side] = jnp.zeros((rows, width), jnp.bfloat16)
            dq_in[side] = jnp.zeros((rows, width), jnp.bfloat16)
            fin_in[side] = jnp.zeros((groups, 3 * group_heads, rows), jnp.float32)
            stat_in[side, :, :group_heads] = jnp.full(
                (groups, group_heads, rows), LOW, jnp.float32
            )
            stat_in[side, :, group_heads:] = jnp.zeros(
                (groups, 2 * group_heads, rows), jnp.float32
            )

    zeros = jnp.zeros((rows, HEAD_DIM), jnp.float32)

    def inverse_scale_of(raw_ref):
        def square_step(g, total):
            for j in range(group_heads):
                block = raw_ref[:, columns(g * group_heads + j)].astype(jnp.float32)
                total = total + block * block
            return total

        total = lax.fori_loop(0, groups, square_step, zeros)
        return 1.0 / jnp.sqrt(jnp.sum(total, axis=1, keepdims=True) / width + 1e-06)

    loads[0].wait()
    q_inv = inverse_scale_of(q_ref)
    loads[1].wait()
    k_inv = inverse_scale_of(k_ref)

    for peer in fsdp_peers:
        for row in range(2):
            gain_copy(row, peer, peer).wait()
    if not aligned:
        for row in range(2):
            gains = gslots[row, 0]
            for i in range(1, fsdp_n):
                gains = gains + gslots[row, i]
            gain[row] = gains

    def head_gain(row, h):
        return gain[row, :, columns(h)]

    def normalize(raw_ref, row, inverse, out):
        @pl.loop(0, groups)
        def _(g):
            for j in range(group_heads):
                cols = columns(g * group_heads + j)
                out[:, cols] = (
                    raw_ref[:, cols].astype(jnp.float32)
                    * inverse
                    * head_gain(row, g * group_heads + j)
                ).astype(jnp.bfloat16)

    normalize(q_ref, 0, q_inv, qn)

    def second_sends(side):
        for g in range(ahead):
            q_chunk(False, side, g).start()

    each_side(second_sends)
    normalize(k_ref, 1, k_inv, kn)

    lane_tile = lax.broadcasted_iota(jnp.int32, (1, rows), 1) // TILE

    @pl.loop(0, heads)
    def _(h):
        for slot in range(3):
            slab = jnp.clip(z + (slot - 1), 0, seq_n - 1)
            real = 1 if slot == 1 else here[slot // 2].astype(jnp.int32)
            for key_tile in range(slab_tiles):
                target = z * slab_tiles + key_tile
                line = jnp.zeros((1, rows), jnp.float32)
                for query_tile in range(slab_tiles):
                    hits = 0
                    for i in range(list_len):
                        picked = lists_ref[i, slab * slab_tiles + query_tile, h]
                        hits = hits + (picked == target).astype(jnp.int32)
                    hits = (hits * real).astype(jnp.float32)
                    line = jnp.where(lane_tile == query_tile, hits, line)
                at = slot * slab_tiles + key_tile
                mask[h, at : at + 1] = line

    loads[2].wait()
    loads[3].wait()

    def stats_of(slot, g, j, queries, cots):
        h = g * group_heads + j
        cols = columns(h)
        scores = dot(kn[:, cols], queries, NT) * score_scale
        probs = dot(v_ref[:, cols], cots, NT)
        live = (
            jnp.concatenate(
                [
                    jnp.broadcast_to(
                        mask[h, slot * slab_tiles + t : slot * slab_tiles + t + 1], (TILE, rows)
                    )
                    for t in range(slab_tiles)
                ],
                axis=0,
            )
            > 0.5
        )
        scores = jnp.where(live, scores, LOW)
        top = jnp.max(scores, axis=0, keepdims=True)
        expo = jnp.where(live, jnp.exp(scores - top), 0.0)
        s_buf[slot, h] = scores
        p_buf[slot, h] = probs
        stat[slot, g, j : j + 1] = top
        stat[slot, g, group_heads + j : group_heads + j + 1] = jnp.sum(
            expo, axis=0, keepdims=True
        )
        stat[slot, g, 2 * group_heads + j : 2 * group_heads + j + 1] = jnp.sum(
            expo * probs, axis=0, keepdims=True
        )

    def back_of(slot, g, j, final, queries, cots):
        h = g * group_heads + j
        top = final[j : j + 1]
        inverse = final[group_heads + j : group_heads + j + 1]
        delta = final[2 * group_heads + j : 2 * group_heads + j + 1]
        weights = jnp.exp(s_buf[slot, h] - top) * inverse
        grads = (weights * (p_buf[slot, h] - delta) * score_scale).astype(jnp.bfloat16)
        return (
            dot(grads, kn[:, columns(h)], TN),
            dot(grads, queries, NN),
            dot(weights.astype(jnp.bfloat16), cots, NN),
        )

    def stats_stage(g):
        for j in range(group_heads):
            cols = columns(g * group_heads + j)
            stats_of(1, g, j, qn[:, cols], c_ref[:, cols])

        def arrive(side):
            c_chunk(True, side, g).wait_recv()
            q_chunk(True, side, g).wait_recv()

        each_side(arrive)
        for j in range(group_heads):
            cols = columns(g * group_heads + j)
            for side in range(2):
                stats_of(2 * side, g, j, hq[side, :, cols], hc[side, :, cols])
        each_side(lambda side: stat_chunk(False, side, g).start())

    def merge_stage(g):
        each_side(lambda side: stat_chunk(True, side, g).wait_recv())
        parts = (stat_in[0, g], stat[1, g], stat_in[1, g])
        tops = [part[:group_heads] for part in parts]
        top = jnp.maximum(jnp.maximum(tops[0], tops[1]), tops[2])
        factors = [jnp.exp(part - top) for part in tops]
        total = sum(p[group_heads : 2 * group_heads] * w for p, w in zip(parts, factors))
        weighted = sum(p[2 * group_heads :] * w for p, w in zip(parts, factors))
        inverse = 1.0 / total
        fin[g, :group_heads] = top
        fin[g, group_heads : 2 * group_heads] = inverse
        fin[g, 2 * group_heads :] = weighted * inverse
        each_side(lambda side: fin_chunk(False, side, g).start())

    def back_stage(g):
        each_side(lambda side: fin_chunk(True, side, g).wait_recv())
        finals = (fin_in[0, g], fin[g], fin_in[1, g])
        for j in range(group_heads):
            cols = columns(g * group_heads + j)
            left = back_of(0, g, j, finals[0], hq[0, :, cols], hc[0, :, cols])
            right = back_of(2, g, j, finals[2], hq[1, :, cols], hc[1, :, cols])
            own = back_of(1, g, j, finals[1], qn[:, cols], c_ref[:, cols])
            dq_send[0, :, cols] = left[0].astype(jnp.bfloat16)
            dq_send[1, :, cols] = right[0].astype(jnp.bfloat16)
            dq_own[:, cols] = own[0]
            dk_ref[:, cols] = (left[1] + right[1] + own[1]).astype(jnp.bfloat16)
            dv_ref[:, cols] = (left[2] + right[2] + own[2]).astype(jnp.bfloat16)
            h = g * group_heads + j
            q_terms = (
                left[0] * hq[0, :, cols].astype(jnp.float32)
                + right[0] * hq[1, :, cols].astype(jnp.float32)
                + own[0] * qn[:, cols].astype(jnp.float32)
            )
            k_terms = dk_ref[:, cols].astype(jnp.float32) * kn[:, cols].astype(jnp.float32)
            gp[0, :, cols] = jnp.sum(q_terms, axis=0, keepdims=True) / head_gain(0, h)
            gp[1, :, cols] = jnp.sum(k_terms, axis=0, keepdims=True) / head_gain(1, h)
        each_side(lambda side: dq_chunk(False, side, g).start())

    @pl.loop(0, groups + 2)
    def _(i):
        @pl.when(i < groups)
        def _():
            stats_stage(i)

        @pl.when(jnp.logical_and(i >= 1, i <= groups))
        def _():
            merge_stage(i - 1)

        @pl.when(i >= 2)
        def _():
            back_stage(i - 2)

        @pl.when(i + ahead < groups)
        def _():
            def more(side):
                c_chunk(False, side, i + ahead).start()
                q_chunk(False, side, i + ahead).start()

            each_side(more)

    def inner_step(row, raw_ref, inverse, g, inner, grad_of):
        for j in range(group_heads):
            h = g * group_heads + j
            cols = columns(h)
            raw = raw_ref[:, cols].astype(jnp.float32)
            grad = grad_of(cols)
            inner = inner + raw * (grad * head_gain(row, h))
        return inner

    def finish(row, raw_ref, out_ref, inverse, inner):
        inner = jnp.sum(inner, axis=1, keepdims=True)
        ratio = inner / width * (inverse * inverse * inverse)

        @pl.loop(0, groups)
        def _(g):
            for j in range(group_heads):
                h = g * group_heads + j
                cols = columns(h)
                raw = raw_ref[:, cols].astype(jnp.float32)
                grad = out_ref[:, cols].astype(jnp.float32)
                out_ref[:, cols] = (
                    grad * head_gain(row, h) * inverse - raw * ratio
                ).astype(jnp.bfloat16)

    def gain_piece(i):
        if aligned:
            return gp.at[:, :, pl.ds(pl.multiple_of(i * share, 128), share)]
        return gp

    def fold_copy(owner, peer):
        return peer_copy(
            gain_piece(peer), fslots.at[owner], f_send.at[peer], f_recv.at[owner], {"fsdp": peer}
        )

    def spread_copy(owner, peer):
        return peer_copy(
            gp2, cslots.at[owner], x_send.at[peer], x_recv.at[owner], row_id(peer)
        )

    outs = [
        pltpu.make_async_copy(src, dst, out_sem.at[i])
        for i, (src, dst) in enumerate(((dq_ref, dq_out), (dk_ref, dk_out), (dv_ref, dv_out)))
    ]
    for peer in fsdp_peers:
        fold_copy(f, peer).start()
    fslots[f] = gain_piece(f)[...]
    outs[2].start()

    inner = lax.fori_loop(
        0,
        groups,
        lambda g, inner: inner_step(
            1, k_ref, k_inv, g, inner, lambda cols: dk_ref[:, cols].astype(jnp.float32)
        ),
        zeros,
    )

    for peer in fsdp_peers:
        fold_copy(peer, peer).wait()
    part = fslots[0]
    for i in range(1, fsdp_n):
        part = part + fslots[i]
    gp2[...] = part
    for peer in row_peers:
        spread_copy(place, peer).start()
    cslots[place] = part

    finish(1, k_ref, dk_ref, k_inv, inner)
    outs[1].start()

    def join_step(g, inner):
        each_side(lambda side: dq_chunk(True, side, g).wait_recv())

        def joined(cols):
            total = (
                dq_own[:, cols]
                + dq_in[0, :, cols].astype(jnp.float32)
                + dq_in[1, :, cols].astype(jnp.float32)
            ).astype(jnp.bfloat16)
            dq_ref[:, cols] = total
            return total.astype(jnp.float32)

        return inner_step(0, q_ref, q_inv, g, inner, joined)

    inner = lax.fori_loop(0, groups, join_step, zeros)
    finish(0, q_ref, dq_ref, q_inv, inner)
    outs[0].start()

    for peer in row_peers:
        spread_copy(peer, peer).wait()
    part = cslots[0]
    for i in range(1, seq_n * cfg_n):
        part = part + cslots[i]
    sum_ref[...] = part / (2.0 * fsdp_n)

    def drain(side):
        @pl.loop(0, groups)
        def _(g):
            for chunk in (c_chunk, q_chunk, stat_chunk, fin_chunk, dq_chunk):
                chunk(False, side, g).wait_send()

    each_side(drain)
    for out in outs:
        out.wait()


def move(*refs):
    sources, sums, targets, lines, buffers = refs[:3], refs[3], refs[4:7], refs[7:9], refs[9:]
    pieces = 4
    step = sources[0].shape[0] // pieces

    def with_sems(in_sem, out_sem):
        reads = []
        writes = []
        for i, (src, dst, buf) in enumerate(zip(sources, targets, buffers)):
            for n in range(pieces):
                part = pl.ds(n * step, step)
                reads.append(
                    pltpu.make_async_copy(src.at[part], buf.at[part], in_sem.at[i, n])
                )
                writes.append(
                    pltpu.make_async_copy(buf.at[part], dst.at[part], out_sem.at[i, n])
                )
        for read in reads:
            read.start()
        for row in range(2):
            lines[row][...] = sums[row]
        for read, write in zip(reads, writes):
            read.wait()
            write.start()
        for write in writes:
            write.wait()

    dma = pltpu.SemaphoreType.DMA((3, pieces))
    pl.run_scoped(with_sems, dma, dma)


def on_device(q_raw, k_raw, value_in, cotangent, q_gain, k_gain, tile_lists):
    seq_n, cfg_n, fsdp_n = (lax.axis_size(name) for name in ("seq", "cfg", "fsdp"))
    rows, width = q_raw.shape[2:]
    heads = width // HEAD_DIM
    share = q_gain.shape[0]
    group_heads = next(n for n in (5, 4, 3, 2, 1) if heads % n == 0)
    groups = heads // group_heads
    aligned = share % 128 == 0
    start = lax.axis_index("fsdp") * share

    def own_gain(gain):
        if aligned:
            return gain[None]
        owner = lax.broadcasted_iota(jnp.int32, (1, width), 1) // share
        return jnp.where(owner == lax.axis_index("fsdp"), jnp.tile(gain, fsdp_n)[None], 0.0)

    bf16, f32 = jnp.bfloat16, jnp.float32
    dma = pltpu.SemaphoreType.DMA
    places = seq_n * cfg_n
    piece = share if aligned else width
    vmem = pl.BlockSpec(memory_space=pltpu.VMEM)
    hbm = pl.BlockSpec(memory_space=pltpu.HBM)
    grad = jax.ShapeDtypeStruct((rows, width), bf16)
    slab = pltpu.VMEM((rows, width), bf16)
    slabs = pltpu.VMEM((2, rows, width), bf16)
    lines = 3 * group_heads
    q_out, k_out, v_out, gain_sums = pl.pallas_call(
        functools.partial(fused, (seq_n, cfg_n, fsdp_n, heads, group_heads, share)),
        out_shape=(grad, grad, grad, jax.ShapeDtypeStruct((2, 1, piece), f32)),
        in_specs=[hbm] * 4 + [vmem] * 2 + [pl.BlockSpec(memory_space=pltpu.SMEM)],
        out_specs=(hbm,) * 3 + (vmem,),
        scratch_shapes=[
            slab,
            slab,
            slab,
            slab,
            slab,
            slab,
            slab,
            slab,
            slab,
            slabs,
            slabs,
            pltpu.VMEM((heads, 3 * (rows // TILE), rows), f32),
            pltpu.VMEM((3, heads, rows, rows), f32),
            pltpu.VMEM((3, heads, rows, rows), f32),
            pltpu.VMEM((3, groups, lines, rows), f32),
            pltpu.VMEM((2, groups, lines, rows), f32),
            pltpu.VMEM((groups, lines, rows), f32),
            pltpu.VMEM((2, groups, lines, rows), f32),
            pltpu.VMEM((rows, width), f32),
            slabs,
            slabs,
            pltpu.VMEM((2, 1, width), f32),
            pltpu.VMEM((2, 1, 1, 128) if aligned else (2, fsdp_n, 1, width), f32),
            pltpu.VMEM((2, 1, width), f32),
            pltpu.VMEM((fsdp_n, 2, 1, piece), f32),
            pltpu.VMEM((2, 1, piece), f32),
            pltpu.VMEM((places, 2, 1, piece), f32),
            dma((4,)),
            dma((3,)),
        ]
        + [dma((2, groups))] * 10
        + [dma((2, fsdp_n))] * 2
        + [dma((fsdp_n,))] * 2
        + [dma((places,))] * 2,
        compiler_params=pltpu.CompilerParams(
            collective_id=0, has_side_effects=True, vmem_limit_bytes=62 * 1024 * 1024
        ),
    )(
        cotangent[0, 0],
        q_raw[0, 0],
        k_raw[0, 0],
        value_in[0, 0],
        own_gain(q_gain),
        own_gain(k_gain),
        tile_lists.transpose(2, 1, 0),
    )
    line = jax.ShapeDtypeStruct((1, piece), f32)
    q_out, k_out, v_out, q_sum, k_sum = pl.pallas_call(
        move,
        out_shape=(grad,) * 3 + (line,) * 2,
        in_specs=[hbm] * 3 + [vmem],
        out_specs=(hbm,) * 3 + (vmem,) * 2,
        scratch_shapes=[slab] * 3,
    )(q_out, k_out, v_out, gain_sums)
    q_sum, k_sum = q_sum[0], k_sum[0]
    if not aligned:
        q_sum = lax.dynamic_slice_in_dim(q_sum, start, share, 0)
        k_sum = lax.dynamic_slice_in_dim(k_sum, start, share, 0)
    return (q_out[None, None], k_out[None, None], v_out[None, None], q_sum, k_sum)


def solution(mesh):
    tokens = P("fsdp", "cfg", "seq", None)
    return jax.shard_map(
        on_device,
        mesh=mesh,
        in_specs=(tokens, tokens, tokens, tokens, P("fsdp"), P("fsdp"), P()),
        out_specs=(tokens, tokens, tokens, P("fsdp"), P("fsdp")),
        check_vma=False,
    )
```
